512 devices in a mesh: leaf: 32 (over z, x), group: 16 (over y, core).
Axes of the slice: x: 4, y: 8, z: 8, core: 2. Of those that a mesh axis runs over, the one named last changes fastest.
Arguments:
- low_solved: float32 [262144, 256], P(('group', 'leaf')), may hold values from -4 to 4, as said below
- low_basis: float32 [262144, 256], P(('group', 'leaf')), may hold values from -0.001933495 to 0.001933495, as said below
- upper_solved: float32 [262144, 512], P(('group', 'leaf')), may hold values from -4 to 4, as said below
- upper_basis: float32 [262144, 256], P(('group', 'leaf')), may hold values from -0.001171875 to 0.001171875, as said below
Outputs:
- pair_solved: float32 [262144, 256], P(('group', 'leaf'))
- next_solved: float32 [262144, 256], P(('group', 'leaf'))
The draws below stay inside these ranges and needn't reach their ends.
Inputs may be any that keep to these rules, and one draw needn't show every extreme that they name: `low_solved`: independent entries of mean zero. `low_basis`: independent entries of mean zero. `upper_solved`: independent entries of mean zero. `upper_basis`: independent entries of mean zero.
All inputs are finite; a program needn't handle non-finite values.
Results may differ from the reference program's by a relative error of at most 0.0003.
Values sent between devices are 32-bit elements; how exact they have to be, the bound alone decides.
A program may use at most 64 MiB of HBM per device.

```python
import jax
import jax.numpy as jnp
from jax import lax

RANK = 256
ITERS = 4
HALF_ROWS = 8192
GROUP_ROWS = 16384
TOTAL_ROWS = 262144
N_GROUP = 16


def spread_draw(key, shape, scale):
    return jnp.clip(jax.random.normal(key, shape, jnp.float32), -4.0, 4.0) * scale


def draw_low_solved(key, part):
    return spread_draw(key, (TOTAL_ROWS, RANK), 1.0)


def draw_low_basis(key, part):
    return spread_draw(key, (TOTAL_ROWS, RANK), 0.7 / (RANK * HALF_ROWS) ** 0.5)


def draw_upper_solved(key, part):
    return spread_draw(key, (TOTAL_ROWS, 2 * RANK), 1.0)


def draw_upper_basis(key, part):
    return spread_draw(key, (TOTAL_ROWS, RANK), 0.6 / (RANK * GROUP_ROWS) ** 0.5)


def setup_inputs(seed: int = 0) -> dict:
    seeds = jax.random.split(jax.random.key(seed), 5)
    return {
        "low_solved": draw_low_solved(jax.random.fold_in(seeds[4], 71), 0),
        "low_basis": draw_low_basis(jax.random.fold_in(seeds[4], 71), 0),
        "upper_solved": draw_upper_solved(jax.random.fold_in(seeds[4], 71), 0),
        "upper_basis": draw_upper_basis(jax.random.fold_in(seeds[4], 71), 0),
    }


def product(left, right):
    return jnp.dot(left, right, precision=lax.Precision.HIGHEST, preferred_element_type=jnp.float32)


def transposed_product(left, right):
    return lax.dot_general(left, right, (((0,), (0,)), ((), ())), precision=lax.Precision.HIGHEST, preferred_element_type=jnp.float32)


def jacobi(couple_first, rhs_first, couple_second, rhs_second):
    update_first = jnp.zeros(rhs_second.shape, jnp.float32)
    update_second = jnp.zeros(rhs_first.shape, jnp.float32)
    for sweep_index in range(ITERS):
        update_first, update_second = rhs_second - product(couple_second, update_second), rhs_first - product(couple_first, update_first)
    return update_first, update_second


def level_group(y_halves, v_halves, z_halves):
    totals = []
    for half_index in range(2):
        joined = jnp.concatenate([y_halves[half_index], z_halves[half_index]], axis=1)
        totals.append(transposed_product(v_halves[half_index], joined))
    update_first, update_second = jacobi(totals[0][:, :RANK], totals[0][:, RANK:], totals[1][:, :RANK], totals[1][:, RANK:])
    middle_first = z_halves[0] - product(y_halves[0], update_first)
    middle_second = z_halves[1] - product(y_halves[1], update_second)
    return jnp.stack([middle_first, middle_second])


def per_pair(pieces):
    y_pair, v_pair, z_pair, w_pair = pieces
    middles = []
    blocks = []
    for group_index in range(2):
        middle = level_group(y_pair[group_index], v_pair[group_index], z_pair[group_index])
        middles.append(middle)
        blocks.append(transposed_product(w_pair[group_index, 0], middle[0]) + transposed_product(w_pair[group_index, 1], middle[1]))
    pair_first, pair_second = jacobi(blocks[0][:, :RANK], blocks[0][:, RANK:], blocks[1][:, :RANK], blocks[1][:, RANK:])
    updates = [pair_first, pair_second]
    solved_rows = []
    next_rows = []
    for group_index in range(2):
        middle = middles[group_index]
        solved = middle[:, :, :RANK]
        nexts = middle[:, :, RANK:] - jnp.stack([product(solved[0], updates[group_index]), product(solved[1], updates[group_index])])
        solved_rows.append(solved)
        next_rows.append(nexts)
    return jnp.stack(solved_rows), jnp.stack(next_rows)


def reference(low_solved, low_basis, upper_solved, upper_basis):
    pairs = N_GROUP // 2
    def split_rows(array):
        return array.reshape(pairs, 2, 2, HALF_ROWS, array.shape[1])
    solved, nexts = lax.map(per_pair, (split_rows(low_solved), split_rows(low_basis), split_rows(upper_solved), split_rows(upper_basis)))
    return solved.reshape(TOTAL_ROWS, RANK), nexts.reshape(TOTAL_ROWS, RANK)
```

```python
import jax
import jax.numpy as jnp
from jax import lax
from jax.experimental import pallas as pl
from jax.experimental.pallas import tpu as pltpu
from jax.sharding import PartitionSpec as P

MESH = pl.DeviceIdType.MESH
NX = 4
NZ = 8
F32 = jnp.float32
BF16 = jnp.bfloat16
N_MESSAGES = 80


def split(value):
    high = value.astype(BF16)
    return high, (value - high.astype(F32)).astype(BF16)


def dot3(left, right):
    left_high, left_low = left
    right_high, right_low = right
    total = jnp.dot(left_high, right_high, preferred_element_type=F32)
    total += jnp.dot(left_high, right_low, preferred_element_type=F32)
    return total + jnp.dot(left_low, right_high, preferred_element_type=F32)


def kernel(
    y_hbm, v_hbm, z_hbm, w_hbm, pair_hbm, next_hbm,
    y_ref, v_ref, z_ref, w_ref, pair_ref, next_ref,
    part_g, part_p, part_q, part_s,
    first_g, first_p, first_q, first_s,
    second_g, second_p, second_q, second_s,
    slice_g, slice_p, slice_q, slice_s,
    peers_g, peers_p, peers_q, peers_s,
    full_g, full_p, table_q, table_s,
    full_u, full_e, sibling_e,
    local_sem, send_sem, recv_sem,
):
    rank = y_ref.shape[1]
    lanes = rank // 2
    rows_l = rank // NX // 4
    rows_q = rank // 4
    leaf = lax.axis_index("leaf")
    group = lax.axis_index("group")
    z, x = leaf // NX, leaf % NX
    half, place = z // 4, z % 4
    flip = x + 1 - 2 * (x % 2)
    mirror = NX - 1 - x
    right, left = (x + 1) % NX, (x + NX - 1) % NX
    up, down = (z + 1) % NZ, (z + NZ - 1) % NZ
    sibling = group + 1 - 2 * (group % 2)

    copies = []
    for index, (source, target) in enumerate(((v_hbm, v_ref), (y_hbm, y_ref), (w_hbm, w_ref), (z_hbm, z_ref))):
        copy = pltpu.make_async_copy(source, target, local_sem.at[index])
        copy.start()
        copies.append(copy)

    barrier = pltpu.get_barrier_semaphore()
    partners = [(z, right), (z, left), (up, x), (down, x)]
    partners += [(half * 4 + (place + d) % 4, x) for d in (1, 2, 3)]
    for pz, px in partners:
        pl.semaphore_signal(barrier, inc=1, device_id={"leaf": pz * NX + px}, device_id_type=MESH)
    pl.semaphore_signal(barrier, inc=1, device_id={"group": sibling}, device_id_type=MESH)

    sent = []

    def send(source, target, device):
        index = len(sent)
        copy = pltpu.make_async_remote_copy(
            src_ref=source,
            dst_ref=target,
            send_sem=send_sem.at[index],
            recv_sem=recv_sem.at[index],
            device_id=device,
            device_id_type=MESH,
        )
        copy.start()
        sent.append(copy)
        return copy

    def at(pz, px):
        return {"leaf": pz * NX + px}

    def reduce_flow(colour, part, first, second, sliced, peers, table):
        if colour == 0:
            one, two = flip, mirror
            keep = 2 * ((x + 1) // 2 % 2)
            own, away = (x + 1) % NX, (mirror + 1) % NX
        else:
            one, two = mirror, flip
            keep = 2 * (x // 2)
            own, away = x, flip
        step_one = send(part.at[pl.ds(2 - keep, 2)], first, at(z, one))
        yield
        step_one.wait_recv()
        part[away] = part[away] + first[away - keep]
        step_two = send(part.at[away], second, at(z, two))
        sliced[...] = part[own] + first[own - keep]
        yield
        step_two.wait_recv()
        sliced[...] = sliced[...] + second[...]
        waits = []
        for d in (1, 2, 3):
            other = (place + d) % 4
            waits.append(send(sliced.at[other], peers.at[d - 1], at(half * 4 + other, x)))
        yield
        for wait in waits:
            wait.wait_recv()
        table[z] = (sliced[place] + peers[0]) + (peers[1] + peers[2])
        n_up, n_down = (4, 3) if colour == 0 else (3, 4)
        going_up = send(table.at[z], table.at[z], at(up, x))
        going_down = send(table.at[z], table.at[z], at(down, x))
        for k in range(1, 5):
            yield
            if k <= n_up:
                going_up.wait_recv()
                if k < n_up:
                    slot = (z + NZ - k) % NZ
                    going_up = send(table.at[slot], table.at[slot], at(up, x))
            if k <= n_down:
                going_down.wait_recv()
                if k < n_down:
                    slot = (z + k) % NZ
                    going_down = send(table.at[slot], table.at[slot], at(down, x))

    def gather_x(full):
        n = full.shape[1] // 2
        to_right = send(full.at[x], full.at[x], at(z, right))
        to_left = send(full.at[x], full.at[x], at(z, left))
        yield
        to_right.wait_recv()
        far_right = send(full.at[left, pl.ds(0, n)], full.at[left, pl.ds(0, n)], at(z, right))
        to_left.wait_recv()
        far_left = send(full.at[right, pl.ds(n, n)], full.at[right, pl.ds(n, n)], at(z, left))
        yield
        far_right.wait_recv()
        far_left.wait_recv()

    def run(flow):
        return next(flow, None)

    copies[0].wait()
    left_v = split(v_ref[...].T)
    copies[1].wait()
    y_parts = split(y_ref[...])

    def put_l(part, value, shift):
        for s in range(NX):
            for j in range(4):
                row = s * 4 * rows_l + j * rows_l
                part[(s + shift) % NX, j, pl.ds(0, rows_l)] = value[row : row + rows_l, :lanes]
                part[(s + shift) % NX, j, pl.ds(rows_l, rows_l)] = value[row : row + rows_l, lanes:]

    def put_q(part, value, slots):
        for n, slot in enumerate(slots):
            for j in range(4):
                part[slot, j] = value[j * rows_q : (j + 1) * rows_q, n * lanes : (n + 1) * lanes]

    put_l(part_g, dot3(left_v, y_parts), 1)
    pl.semaphore_wait(barrier, len(partners) + 1)
    flow_g = reduce_flow(0, part_g, first_g, second_g, slice_g, peers_g, full_g.at[x])
    run(flow_g)
    copies[2].wait()
    left_w = split(w_ref[...].T)
    put_l(part_p, dot3(left_w, y_parts), 0)
    flow_p = reduce_flow(1, part_p, first_p, second_p, slice_p, peers_p, full_p.at[x])
    run(flow_p)
    copies[3].wait()
    z_pair = split(z_ref[:, :rank])
    z_next = split(z_ref[:, rank:])
    put_q(part_q, dot3(left_v, z_pair), (1, 2))
    put_q(part_q, dot3(left_v, z_next), (3, 0))
    flow_q = reduce_flow(0, part_q, first_q, second_q, slice_q, peers_q, table_q)
    run(flow_q)
    put_q(part_s, dot3(left_w, z_pair), (0, 1))
    put_q(part_s, dot3(left_w, z_next), (2, 3))
    flow_s = reduce_flow(1, part_s, first_s, second_s, slice_s, peers_s, table_s)
    run(flow_s)

    small, large = (flow_g, flow_p), (flow_q, flow_s)
    for flow in small:
        run(flow)
    for flow in small:
        run(flow)
    for flow in large:
        run(flow)
    for flow in small:
        run(flow)
    for flow in large:
        run(flow)
    for step in range(4):
        for flow in small:
            run(flow)
        if step == 1:
            for flow in large:
                run(flow)
    gathers = gather_x(full_g), gather_x(full_p)
    for flow in gathers:
        run(flow)
    for step in range(2):
        for flow in large:
            run(flow)
    for flow in gathers:
        run(flow)
    for step in range(2):
        for flow in large:
            run(flow)
    for flow in gathers:
        run(flow)

    def whole(full, h):
        block = full[:, pl.ds(4 * h, 4)]
        halves = [block[:, :, n * rows_l : (n + 1) * rows_l].reshape(rank, lanes) for n in range(2)]
        return jnp.concatenate(halves, axis=1)

    mine, others = half, 1 - half
    g_own, g_other = split(whole(full_g, mine)), split(whole(full_g, others))
    q_own = table_q[pl.ds(4 * mine, 4)].reshape(rank, lanes)
    q_other = table_q[pl.ds(4 * others, 4)].reshape(rank, lanes)
    u_own, u_other = q_other, q_own
    for sweep in range(3):
        u_own, u_other = (
            q_other - dot3(g_other, split(u_other)),
            q_own - dot3(g_own, split(u_own)),
        )
    full_u[x] = u_own.reshape(4, rows_q, lanes)
    flow_u = gather_x(full_u)
    run(flow_u)
    p_own, p_other = split(whole(full_p, mine)), split(whole(full_p, others))
    total_s = (table_s[pl.ds(0, 4)] + table_s[pl.ds(4, 4)]).reshape(rank, lanes)
    e_slice = total_s - dot3(p_own, split(u_own)) - dot3(p_other, split(u_other))
    full_e[x] = e_slice.reshape(4, rows_q, lanes)
    across = {"group": sibling}
    flow_e = gather_x(full_e)
    run(flow_e)
    shared = [send(full_e.at[x], sibling_e.at[x], across)]
    run(flow_u)
    run(flow_e)
    for slot in (left, right):
        shared.append(send(full_e.at[slot], sibling_e.at[slot], across))
    run(flow_u)

    y_parts = split(y_ref[...])

    def joined(full, first_slot):
        return jnp.concatenate([full[first_slot + n].reshape(rank, lanes) for n in range(2)], axis=1)

    pair = z_ref[:, :rank] - dot3(y_parts, split(joined(full_u, 0)))
    pair_ref[...] = pair
    pair_out = pltpu.make_async_copy(pair_ref, pair_hbm, local_sem.at[4])
    pair_out.start()
    middle_next = z_ref[:, rank:] - dot3(y_parts, split(joined(full_u, 2)))
    run(flow_e)
    far = (x + 2) % NX
    shared.append(send(full_e.at[far], sibling_e.at[far], across))
    for copy in shared:
        copy.wait_recv()
    b_own, r_own = split(joined(full_e, 0)), joined(full_e, 2)
    b_sibling, r_sibling = split(joined(sibling_e, 0)), joined(sibling_e, 2)
    update = r_own
    update = r_sibling - dot3(b_sibling, split(update))
    update = r_own - dot3(b_own, split(update))
    update = r_sibling - dot3(b_sibling, split(update))
    next_ref[...] = middle_next - dot3(split(pair), split(update))
    next_out = pltpu.make_async_copy(next_ref, next_hbm, local_sem.at[5])
    next_out.start()
    for copy in sent:
        copy.wait_send()
    pair_out.wait()
    next_out.wait()


def body(low_solved, low_basis, upper_solved, upper_basis):
    rows, rank = low_solved.shape
    lanes, rows_l, rows_q = rank // 2, rank // NX // 4, rank // 4
    heights = (2 * rows_l, 2 * rows_l, rows_q, rows_q)

    def blocks(*lead):
        return [pltpu.VMEM((*lead, height, lanes), F32) for height in heights]

    scratch = [
        pltpu.VMEM((rows, rank), F32),
        pltpu.VMEM((rows, rank), F32),
        pltpu.VMEM((rows, 2 * rank), F32),
        pltpu.VMEM((rows, rank), F32),
        pltpu.VMEM((rows, rank), F32),
        pltpu.VMEM((rows, rank), F32),
        *blocks(NX, 4),
        *blocks(2, 4),
        *blocks(4),
        *blocks(4),
        *blocks(3),
        pltpu.VMEM((NX, NZ, 2 * rows_l, lanes), F32),
        pltpu.VMEM((NX, NZ, 2 * rows_l, lanes), F32),
        pltpu.VMEM((NZ, rows_q, lanes), F32),
        pltpu.VMEM((NZ, rows_q, lanes), F32),
        pltpu.VMEM((NX, 4, rows_q, lanes), F32),
        pltpu.VMEM((NX, 4, rows_q, lanes), F32),
        pltpu.VMEM((NX, 4, rows_q, lanes), F32),
        pltpu.SemaphoreType.DMA((6,)),
        pltpu.SemaphoreType.DMA((N_MESSAGES,)),
        pltpu.SemaphoreType.DMA((N_MESSAGES,)),
    ]
    out = jax.ShapeDtypeStruct((rows, rank), F32)
    return pl.pallas_call(
        kernel,
        out_shape=(out, out),
        in_specs=[pl.BlockSpec(memory_space=pl.ANY)] * 4,
        out_specs=[pl.BlockSpec(memory_space=pl.ANY)] * 2,
        scratch_shapes=scratch,
        compiler_params=pltpu.CompilerParams(collective_id=0, has_side_effects=True, vmem_limit_bytes=60 * 2**20),
        name="lowrank_level",
    )(low_solved, low_basis, upper_solved, upper_basis)


def solution(mesh):
    spec = P(("group", "leaf"), None)
    return jax.shard_map(
        body, mesh=mesh, in_specs=(spec,) * 4, out_specs=(spec,) * 2, check_vma=False
    )
```

```python
import jax
import jax.numpy as jnp
from jax import lax
from jax.experimental import pallas as pl
from jax.experimental.pallas import tpu as pltpu
from jax.sharding import PartitionSpec as P

MESH = pl.DeviceIdType.MESH
NX = 4
NZ = 8
F32 = jnp.float32
BF16 = jnp.bfloat16
N_MESSAGES = 176
X_DIRECT = ""
Z_DIRECT = ""
G_DIRECT = "g"
ORDER = (
    "CG", "xg", "CQ", "xq", "CP", "xg", "CS", "xp", "xq", "xs", "xg", "zg", "xp", "xq", "zq", "zg", "xs", "ag",
    "xp", "zp", "ag", "gn", "xs", "zs", "zp", "zq", "ap", "ag", "aq", "ap", "gn", "pn", "ap", "ag", "gr", "zs",
    "as", "aq", "ap", "pr", "aq", "pn", "as", "as", "pr", "gr", "aq", "U", "as", "pr", "pn", "E", "fu", "ef",
    "en", "fu", "M",
)


def split(value):
    high = value.astype(BF16)
    return high, (value - high.astype(F32)).astype(BF16)


def dot3(left, right):
    left_high, left_low = left
    right_high, right_low = right
    total = jnp.dot(left_high, right_high, preferred_element_type=F32)
    total += jnp.dot(left_high, right_low, preferred_element_type=F32)
    return total + jnp.dot(left_low, right_high, preferred_element_type=F32)


def kernel(
    y_hbm, v_hbm, z_hbm, w_hbm, pair_hbm, next_hbm,
    y_ref, v_ref, z_ref, w_ref, pair_ref, next_ref,
    part_g, part_p, part_q, part_s,
    first_g, first_p, first_q, first_s,
    second_g, second_p, second_q, second_s,
    slice_g, slice_p, slice_q, slice_s,
    peers_g, peers_p, peers_q, peers_s,
    full_g, full_p, table_q, table_s,
    full_u, full_e, sibling_e,
    local_sem, send_sem, recv_sem,
):
    rank = y_ref.shape[1]
    lanes = rank // 2
    rows_l = rank // NX // 4
    rows_q = rank // 4
    leaf = lax.axis_index("leaf")
    group = lax.axis_index("group")
    z, x = leaf // NX, leaf % NX
    half, place = z // 4, z % 4
    flip = x + 1 - 2 * (x % 2)
    mirror = NX - 1 - x
    right, left = (x + 1) % NX, (x + NX - 1) % NX
    sibling = group + 1 - 2 * (group % 2)

    copies = []
    for index, (source, target) in enumerate(((v_hbm, v_ref), (y_hbm, y_ref), (z_hbm, z_ref), (w_hbm, w_ref))):
        copy = pltpu.make_async_copy(source, target, local_sem.at[index])
        if index < 2:
            copy.start()
        copies.append(copy)

    barrier = pltpu.get_barrier_semaphore()
    partners = [(z, right), (z, left), (z, (x + 2) % NX)] + [((z + d + NZ) % NZ, x) for d in (1, -1, 2, -2, 3, -3, 4)]
    for pz, px in partners:
        pl.semaphore_signal(barrier, inc=1, device_id={"leaf": pz * NX + px}, device_id_type=MESH)
    pl.semaphore_signal(barrier, inc=1, device_id={"group": sibling}, device_id_type=MESH)

    sent = []

    def send(source, target, device):
        index = len(sent)
        copy = pltpu.make_async_remote_copy(
            src_ref=source,
            dst_ref=target,
            send_sem=send_sem.at[index],
            recv_sem=recv_sem.at[index],
            device_id=device,
            device_id_type=MESH,
        )
        copy.start()
        sent.append(copy)
        return copy

    def at(pz, px):
        return {"leaf": pz * NX + px}

    def scatter_x(colour, part, first, second, sliced, n, direct):
        if colour == 0:
            one, two = flip, mirror
            keep = 2 * ((x + 1) // 2 % 2)
            own, away = (x + 1) % NX, (mirror + 1) % NX
        else:
            one, two = mirror, flip
            keep = 2 * (x // 2)
            own, away = x, flip
        if direct:
            copies_in = []
            for d, target in ((1, first.at[colour, 0]), (3, first.at[colour, 1]), (2, second.at[colour])):
                px = (x + d) % NX
                copies_in.append(send(part.at[colour, px if colour else (px + 1) % NX], target, at(z, px)))
            yield
            for copy in copies_in:
                copy.wait_recv()
            sliced[:, n] = (part[colour, own] + first[colour, 0]) + (first[colour, 1] + second[colour])
            return
        step_one = send(part.at[colour, pl.ds(2 - keep, 2)], first.at[colour], at(z, one))
        yield
        step_one.wait_recv()
        part[colour, away] = part[colour, away] + first[colour, away - keep]
        step_two = send(part.at[colour, away], second.at[colour], at(z, two))
        sliced[:, n] = part[colour, own] + first[colour, own - keep]
        yield
        step_two.wait_recv()
        sliced[:, n] = sliced[:, n] + second[colour]

    def scatter_z(sliced, peers, put):
        waits = []
        for d in (1, 2, 3):
            other = (place + d) % 4
            waits.append(send(sliced.at[other], peers.at[d - 1], at(half * 4 + other, x)))
        yield
        for wait in waits:
            wait.wait_recv()
        put((sliced[place] + peers[0]) + (peers[1] + peers[2]))

    def gather_z(table, far, slots, direct):
        def pass_on(k, to):
            here, there = slots(k, to)
            return send(table(here), table(there), at((z + to + NZ) % NZ, x))

        near = [pass_on(0, to) for to in (1, -1)]
        second = [pass_on(0, to) for to in (2, -2)]
        if direct:
            second += [pass_on(0, to) for to in (3, -3, 4 * far)]
            yield
            for copy in near:
                copy.wait_recv()
            yield
            yield
            for copy in second:
                copy.wait_recv()
            return
        yield
        for copy in near:
            copy.wait_recv()
        third = [pass_on(-1, 2), pass_on(1, -2)]
        yield
        for copy in second:
            copy.wait_recv()
        third.append(pass_on(-2 * far, 2 * far))
        yield
        for copy in third:
            copy.wait_recv()

    def gather_x(full, pieces, to_right_far, to_left_far, direct=False):
        if direct:
            moves = [send(full.at[x, p], full.at[x, p], at(z, px)) for px in (right, left, (x + 2) % NX) for p in pieces]
            yield
            for copy in moves:
                copy.wait_recv()
            return
        to_right = [send(full.at[x, p], full.at[x, p], at(z, right)) for p in pieces]
        to_left = [send(full.at[x, p], full.at[x, p], at(z, left)) for p in pieces]
        yield
        for copy in to_right:
            copy.wait_recv()
        far_right = send(full.at[left, to_right_far], full.at[left, to_right_far], at(z, right))
        for copy in to_left:
            copy.wait_recv()
        far_left = send(full.at[right, to_left_far], full.at[right, to_left_far], at(z, left))
        yield
        far_right.wait_recv()
        far_left.wait_recv()

    def run(*flows):
        for flow in flows:
            next(flow, None)

    def absolute(k, to):
        slot = (z + k + NZ) % NZ
        return slot, slot

    def relative(k, to):
        return 4 + k, 4 + k - to

    def put_full(full):
        def put(value):
            full[x, 4] = value.reshape(full.shape[2:])
        return put

    def put_table(table):
        def put(value):
            table[z] = value.reshape(table.shape[1:])
        return put

    def put_l(part, value):
        for n in range(2):
            for s in range(NX):
                for j in range(4):
                    row = s * 4 * rows_l + j * rows_l
                    slot = (s + 1) % NX if n == 0 else s
                    part[n, slot, j] = value[row : row + rows_l, n * lanes : (n + 1) * lanes]

    def put_q(part, value, slices):
        for m, s in enumerate(slices):
            for j in range(4):
                for n in range(2):
                    slot = (s + 1) % NX if n == 0 else s
                    row = j * rows_q + n * (rows_q // 2)
                    part[n, slot, j] = value[row : row + rows_q // 2, m * lanes : (m + 1) * lanes]

    def scatters(part, first, second, sliced, name):
        return [scatter_x(n, part, first, second, sliced, n, name in X_DIRECT) for n in range(2)]

    xg = scatters(part_g, first_g, second_g, slice_g, "g")
    xp = scatters(part_p, first_p, second_p, slice_p, "p")
    xq = scatters(part_q, first_q, second_q, slice_q, "q")
    xs = scatters(part_s, first_s, second_s, slice_s, "s")
    zg = scatter_z(slice_g, peers_g, put_full(full_g))
    zp = scatter_z(slice_p, peers_p, put_full(full_p))
    zq = scatter_z(slice_q, peers_q, put_table(table_q))
    zs = scatter_z(slice_s, peers_s, put_table(table_s))
    ag = gather_z(lambda slot: full_g.at[x, slot], 1, relative, "g" in Z_DIRECT)
    ap = gather_z(lambda slot: full_p.at[x, slot], 1, relative, "p" in Z_DIRECT)
    aq = gather_z(lambda slot: table_q.at[slot], -1, absolute, "q" in Z_DIRECT)
    as_ = gather_z(lambda slot: table_s.at[slot], -1, absolute, "s" in Z_DIRECT)

    def near(full, name):
        return gather_x(full, [pl.ds(3, 3)], pl.ds(3, 1), pl.ds(4, 2), name in G_DIRECT)

    def rest(full, name):
        return gather_x(full, [pl.ds(0, 3), pl.ds(6, 2)], pl.ds(0, 3), pl.ds(6, 2), name in G_DIRECT)

    def blocks(full):
        return gather_x(full, [pl.ds(0, 4)], pl.ds(0, 2), pl.ds(2, 2))

    held = {}

    def whole(full, h):
        halves = [[], []]
        for s in range(NX):
            for j in range(4):
                slot = (4 * h + j - z + 4 + NZ) % NZ
                for n in range(2):
                    halves[n].append(full[s, slot, pl.ds(n * rows_l, rows_l)])
        return jnp.concatenate([jnp.concatenate(rows, axis=0) for rows in halves], axis=1)

    def joined(full, first_slot):
        return jnp.concatenate([full[first_slot + n].reshape(rank, lanes) for n in range(2)], axis=1)

    mine, others = half, 1 - half
    across = {"group": sibling}
    shared = []

    def compute_g():
        copies[0].wait()
        held["v"] = split(v_ref[...].T)
        copies[1].wait()
        copies[2].start()
        copies[3].start()
        held["y"] = split(y_ref[...])
        put_l(part_g, dot3(held["v"], held["y"]))
        pl.semaphore_wait(barrier, len(partners) + 1)

    def compute_q():
        copies[2].wait()
        held["pair"] = split(z_ref[:, :rank])
        put_q(part_q, dot3(held["v"], held["pair"]), (0, 1))
        held["next"] = split(z_ref[:, rank:])
        put_q(part_q, dot3(held["v"], held["next"]), (2, 3))

    def compute_p():
        copies[3].wait()
        held["w"] = split(w_ref[...].T)
        put_l(part_p, dot3(held["w"], held["y"]))

    def compute_s():
        put_q(part_s, dot3(held["w"], held["pair"]), (0, 1))
        put_q(part_s, dot3(held["w"], held["next"]), (2, 3))

    flow_u = blocks(full_u)
    far = (x + 2) % NX

    def solve_u():
        g_own, g_other = split(whole(full_g, mine)), split(whole(full_g, others))
        q_own = table_q[pl.ds(4 * mine, 4)].reshape(rank, lanes)
        q_other = table_q[pl.ds(4 * others, 4)].reshape(rank, lanes)
        u_own, u_other = q_other, q_own
        for sweep in range(3):
            u_own, u_other = (
                q_other - dot3(g_other, split(u_other)),
                q_own - dot3(g_own, split(u_own)),
            )
        held["u"] = u_own, u_other
        full_u[x] = u_own.reshape(4, rows_q, lanes)
        run(flow_u)

    def solve_e():
        u_own, u_other = held["u"]
        p_own, p_other = split(whole(full_p, mine)), split(whole(full_p, others))
        total_s = (table_s[pl.ds(0, 4)] + table_s[pl.ds(4, 4)]).reshape(rank, lanes)
        e_slice = total_s - dot3(p_own, split(u_own)) - dot3(p_other, split(u_other))
        full_e[x] = e_slice.reshape(4, rows_q, lanes)
        held["e"] = [send(full_e.at[x], full_e.at[x], at(z, px)) for px in (right, left, far)]
        shared.append(send(full_e.at[x], sibling_e.at[x], across))

    def near_e():
        for copy, slot in zip(held["e"], (left, right)):
            copy.wait_recv()
            shared.append(send(full_e.at[slot], sibling_e.at[slot], across))

    def far_e():
        held["e"][2].wait_recv()
        shared.append(send(full_e.at[far], sibling_e.at[far], across))

    def middle():
        y_parts = split(y_ref[...])
        pair = z_ref[:, :rank] - dot3(y_parts, split(joined(full_u, 0)))
        pair_ref[...] = pair
        pair_out = pltpu.make_async_copy(pair_ref, pair_hbm, local_sem.at[4])
        pair_out.start()
        held["m"] = pair, z_ref[:, rank:] - dot3(y_parts, split(joined(full_u, 2))), pair_out

    actions = {
        "CG": compute_g, "CQ": compute_q, "CP": compute_p, "CS": compute_s,
        "U": solve_u, "E": solve_e, "fu": lambda: run(flow_u), "en": near_e, "ef": far_e, "M": middle,
    }
    flows = {
        "xg": xg, "xq": xq, "xp": xp, "xs": xs, "zg": [zg], "zq": [zq], "zp": [zp], "zs": [zs],
        "ag": [ag], "aq": [aq], "ap": [ap], "as": [as_],
        "gn": [near(full_g, "g")], "gr": [rest(full_g, "g")], "pn": [near(full_p, "p")], "pr": [rest(full_p, "p")],
    }
    for token in ORDER:
        if token in actions:
            actions[token]()
        else:
            run(*flows[token])

    for copy in shared:
        copy.wait_recv()
    pair, middle_next, pair_out = held["m"]
    b_own, r_own = split(joined(full_e, 0)), joined(full_e, 2)
    b_sibling, r_sibling = split(joined(sibling_e, 0)), joined(sibling_e, 2)
    update = r_own
    update = r_sibling - dot3(b_sibling, split(update))
    update = r_own - dot3(b_own, split(update))
    update = r_sibling - dot3(b_sibling, split(update))
    next_ref[...] = middle_next - dot3(split(pair), split(update))
    next_out = pltpu.make_async_copy(next_ref, next_hbm, local_sem.at[5])
    next_out.start()
    for copy in sent:
        copy.wait_send()
    pair_out.wait()
    next_out.wait()


def body(low_solved, low_basis, upper_solved, upper_basis):
    rows, rank = low_solved.shape
    lanes, rows_l, rows_q = rank // 2, rank // NX // 4, rank // 4
    heights = (rows_l, rows_l, rows_q // 2, rows_q // 2)

    def blocks(*lead):
        return [pltpu.VMEM((*lead, height, lanes), F32) for height in heights]

    def pieces(*lead):
        return [pltpu.VMEM((*lead, 2, height, lanes), F32) for height in heights[:2]] + [
            pltpu.VMEM((*lead, 2, height, lanes), F32) for height in heights[2:]
        ]

    scratch = [
        pltpu.VMEM((rows, rank), F32),
        pltpu.VMEM((rows, rank), F32),
        pltpu.VMEM((rows, 2 * rank), F32),
        pltpu.VMEM((rows, rank), F32),
        pltpu.VMEM((rows, rank), F32),
        pltpu.VMEM((rows, rank), F32),
        *blocks(2, NX, 4),
        *blocks(2, 2, 4),
        *blocks(2, 4),
        *pieces(4),
        *pieces(3),
        pltpu.VMEM((NX, NZ, 2 * rows_l, lanes), F32),
        pltpu.VMEM((NX, NZ, 2 * rows_l, lanes), F32),
        pltpu.VMEM((NZ, rows_q, lanes), F32),
        pltpu.VMEM((NZ, rows_q, lanes), F32),
        pltpu.VMEM((NX, 4, rows_q, lanes), F32),
        pltpu.VMEM((NX, 4, rows_q, lanes), F32),
        pltpu.VMEM((NX, 4, rows_q, lanes), F32),
        pltpu.SemaphoreType.DMA((6,)),
        pltpu.SemaphoreType.DMA((N_MESSAGES,)),
        pltpu.SemaphoreType.DMA((N_MESSAGES,)),
    ]
    out = jax.ShapeDtypeStruct((rows, rank), F32)
    return pl.pallas_call(
        kernel,
        out_shape=(out, out),
        in_specs=[pl.BlockSpec(memory_space=pl.ANY)] * 4,
        out_specs=[pl.BlockSpec(memory_space=pl.ANY)] * 2,
        scratch_shapes=scratch,
        compiler_params=pltpu.CompilerParams(collective_id=0, has_side_effects=True, vmem_limit_bytes=60 * 2**20),
        name="lowrank_level",
    )(low_solved, low_basis, upper_solved, upper_basis)


def solution(mesh):
    spec = P(("group", "leaf"), None)
    return jax.shard_map(
        body, mesh=mesh, in_specs=(spec,) * 4, out_specs=(spec,) * 2, check_vma=False
    )
```

```python
import jax
import jax.numpy as jnp
from jax import lax
from jax.experimental import pallas as pl
from jax.experimental.pallas import tpu as pltpu
from jax.sharding import PartitionSpec as P

MESH = pl.DeviceIdType.MESH
NX = 4
NZ = 8
F32 = jnp.float32
BF16 = jnp.bfloat16
N_MESSAGES = 176
X_DIRECT = ""
Z_DIRECT = ""
G_DIRECT = "g"
ORDER = (
    "CG", "xg", "CQ", "xq", "CP", "xg", "CS", "xp", "xq", "xs", "xg", "zg", "xp", "xq", "zq", "zg", "xs", "ag",
    "xp", "zp", "ag", "gn", "xs", "zs", "zp", "zq", "ap", "ag", "aq", "ap", "gn", "pn", "ap", "ag", "gr", "zs",
    "as", "aq", "ap", "pr", "aq", "pn", "as", "as", "pr", "gr", "aq", "U", "as", "pr", "pn", "E", "fu", "en",
    "ef", "W", "fu", "M",
)


def split(value):
    high = value.astype(BF16)
    return high, (value - high.astype(F32)).astype(BF16)


def dot3(left, right):
    left_high, left_low = left
    right_high, right_low = right
    total = jnp.dot(left_high, right_high, preferred_element_type=F32)
    total += jnp.dot(left_high, right_low, preferred_element_type=F32)
    return total + jnp.dot(left_low, right_high, preferred_element_type=F32)


def kernel(
    y_hbm, v_hbm, z_hbm, w_hbm, pair_hbm, next_hbm,
    y_ref, v_ref, z_ref, w_ref, pair_ref, next_ref,
    part_g, part_p, part_q, part_s,
    first_g, first_p, first_q, first_s,
    second_g, second_p, second_q, second_s,
    slice_g, slice_p, slice_q, slice_s,
    peers_g, peers_p, peers_q, peers_s,
    full_g, full_p, table_q, table_s,
    full_u, full_e, sibling_e,
    local_sem, send_sem, recv_sem,
):
    rank = y_ref.shape[1]
    lanes = rank // 2
    rows_l = rank // NX // 4
    rows_q = rank // 4
    leaf = lax.axis_index("leaf")
    group = lax.axis_index("group")
    z, x = leaf // NX, leaf % NX
    half, place = z // 4, z % 4
    flip = x + 1 - 2 * (x % 2)
    mirror = NX - 1 - x
    right, left = (x + 1) % NX, (x + NX - 1) % NX
    sibling = group + 1 - 2 * (group % 2)

    copies = []
    for index, (source, target) in enumerate(((v_hbm, v_ref), (y_hbm, y_ref), (z_hbm, z_ref), (w_hbm, w_ref))):
        copy = pltpu.make_async_copy(source, target, local_sem.at[index])
        if index < 2:
            copy.start()
        copies.append(copy)

    barrier = pltpu.get_barrier_semaphore()
    partners = [(z, right), (z, left), (z, (x + 2) % NX)] + [((z + d + NZ) % NZ, x) for d in (1, -1, 2, -2, 3, -3, 4)]
    for pz, px in partners:
        pl.semaphore_signal(barrier, inc=1, device_id={"leaf": pz * NX + px}, device_id_type=MESH)
    pl.semaphore_signal(barrier, inc=1, device_id={"group": sibling}, device_id_type=MESH)

    sent = []

    def send(source, target, device):
        index = len(sent)
        copy = pltpu.make_async_remote_copy(
            src_ref=source,
            dst_ref=target,
            send_sem=send_sem.at[index],
            recv_sem=recv_sem.at[index],
            device_id=device,
            device_id_type=MESH,
        )
        copy.start()
        sent.append(copy)
        return copy

    def at(pz, px):
        return {"leaf": pz * NX + px}

    def scatter_x(colour, part, first, second, sliced, n, direct):
        if colour == 0:
            one, two = flip, mirror
            keep = 2 * ((x + 1) // 2 % 2)
            own, away = (x + 1) % NX, (mirror + 1) % NX
        else:
            one, two = mirror, flip
            keep = 2 * (x // 2)
            own, away = x, flip
        if direct:
            copies_in = []
            for d, target in ((1, first.at[colour, 0]), (3, first.at[colour, 1]), (2, second.at[colour])):
                px = (x + d) % NX
                copies_in.append(send(part.at[colour, px if colour else (px + 1) % NX], target, at(z, px)))
            yield
            for copy in copies_in:
                copy.wait_recv()
            sliced[:, n] = (part[colour, own] + first[colour, 0]) + (first[colour, 1] + second[colour])
            return
        step_one = send(part.at[colour, pl.ds(2 - keep, 2)], first.at[colour], at(z, one))
        yield
        step_one.wait_recv()
        part[colour, away] = part[colour, away] + first[colour, away - keep]
        step_two = send(part.at[colour, away], second.at[colour], at(z, two))
        sliced[:, n] = part[colour, own] + first[colour, own - keep]
        yield
        step_two.wait_recv()
        sliced[:, n] = sliced[:, n] + second[colour]

    def scatter_z(sliced, peers, put):
        waits = []
        for d in (1, 2, 3):
            other = (place + d) % 4
            waits.append(send(sliced.at[other], peers.at[d - 1], at(half * 4 + other, x)))
        yield
        for wait in waits:
            wait.wait_recv()
        put((sliced[place] + peers[0]) + (peers[1] + peers[2]))

    def gather_z(table, far, slots, direct):
        def pass_on(k, to):
            here, there = slots(k, to)
            return send(table(here), table(there), at((z + to + NZ) % NZ, x))

        near = [pass_on(0, to) for to in (1, -1)]
        second = [pass_on(0, to) for to in (2, -2)]
        if direct:
            second += [pass_on(0, to) for to in (3, -3, 4 * far)]
            yield
            for copy in near:
                copy.wait_recv()
            yield
            yield
            for copy in second:
                copy.wait_recv()
            return
        yield
        for copy in near:
            copy.wait_recv()
        third = [pass_on(-1, 2), pass_on(1, -2)]
        yield
        for copy in second:
            copy.wait_recv()
        third.append(pass_on(-2 * far, 2 * far))
        yield
        for copy in third:
            copy.wait_recv()

    def gather_x(full, pieces, to_right_far, to_left_far, direct=False):
        if direct:
            moves = [send(full.at[x, p], full.at[x, p], at(z, px)) for px in (right, left, (x + 2) % NX) for p in pieces]
            yield
            for copy in moves:
                copy.wait_recv()
            return
        to_right = [send(full.at[x, p], full.at[x, p], at(z, right)) for p in pieces]
        to_left = [send(full.at[x, p], full.at[x, p], at(z, left)) for p in pieces]
        yield
        for copy in to_right:
            copy.wait_recv()
        far_right = send(full.at[left, to_right_far], full.at[left, to_right_far], at(z, right))
        for copy in to_left:
            copy.wait_recv()
        far_left = send(full.at[right, to_left_far], full.at[right, to_left_far], at(z, left))
        yield
        far_right.wait_recv()
        far_left.wait_recv()

    def run(*flows):
        for flow in flows:
            next(flow, None)

    def absolute(k, to):
        slot = (z + k + NZ) % NZ
        return slot, slot

    def relative(k, to):
        return 4 + k, 4 + k - to

    def put_full(full):
        def put(value):
            full[x, 4] = value.reshape(full.shape[2:])
        return put

    def put_table(table):
        def put(value):
            table[z] = value.reshape(table.shape[1:])
        return put

    def put_l(part, value):
        for n in range(2):
            for s in range(NX):
                for j in range(4):
                    row = s * 4 * rows_l + j * rows_l
                    slot = (s + 1) % NX if n == 0 else s
                    part[n, slot, j] = value[row : row + rows_l, n * lanes : (n + 1) * lanes]

    def put_q(part, value, slices):
        for m, s in enumerate(slices):
            for j in range(4):
                for n in range(2):
                    slot = (s + 1) % NX if n == 0 else s
                    row = j * rows_q + n * (rows_q // 2)
                    part[n, slot, j] = value[row : row + rows_q // 2, m * lanes : (m + 1) * lanes]

    def scatters(part, first, second, sliced, name):
        return [scatter_x(n, part, first, second, sliced, n, name in X_DIRECT) for n in range(2)]

    xg = scatters(part_g, first_g, second_g, slice_g, "g")
    xp = scatters(part_p, first_p, second_p, slice_p, "p")
    xq = scatters(part_q, first_q, second_q, slice_q, "q")
    xs = scatters(part_s, first_s, second_s, slice_s, "s")
    zg = scatter_z(slice_g, peers_g, put_full(full_g))
    zp = scatter_z(slice_p, peers_p, put_full(full_p))
    zq = scatter_z(slice_q, peers_q, put_table(table_q))
    zs = scatter_z(slice_s, peers_s, put_table(table_s))
    ag = gather_z(lambda slot: full_g.at[x, slot], 1, relative, "g" in Z_DIRECT)
    ap = gather_z(lambda slot: full_p.at[x, slot], 1, relative, "p" in Z_DIRECT)
    aq = gather_z(lambda slot: table_q.at[slot], -1, absolute, "q" in Z_DIRECT)
    as_ = gather_z(lambda slot: table_s.at[slot], -1, absolute, "s" in Z_DIRECT)

    def near(full, name):
        return gather_x(full, [pl.ds(3, 3)], pl.ds(3, 1), pl.ds(4, 2), name in G_DIRECT)

    def rest(full, name):
        return gather_x(full, [pl.ds(0, 3), pl.ds(6, 2)], pl.ds(0, 3), pl.ds(6, 2), name in G_DIRECT)

    def blocks(full):
        return gather_x(full, [pl.ds(0, 4)], pl.ds(0, 2), pl.ds(2, 2))

    held = {}

    def whole(full, h):
        halves = [[], []]
        for s in range(NX):
            for j in range(4):
                slot = (4 * h + j - z + 4 + NZ) % NZ
                for n in range(2):
                    halves[n].append(full[s, slot, pl.ds(n * rows_l, rows_l)])
        return jnp.concatenate([jnp.concatenate(rows, axis=0) for rows in halves], axis=1)

    def joined(full, first_slot):
        return jnp.concatenate([full[first_slot + n].reshape(rank, lanes) for n in range(2)], axis=1)

    mine, others = half, 1 - half
    across = {"group": sibling}
    shared = []

    def compute_g():
        copies[0].wait()
        held["v"] = split(v_ref[...].T)
        copies[1].wait()
        copies[2].start()
        copies[3].start()
        held["y"] = split(y_ref[...])
        put_l(part_g, dot3(held["v"], held["y"]))
        pl.semaphore_wait(barrier, len(partners) + 1)

    def compute_q():
        copies[2].wait()
        held["pair"] = split(z_ref[:, :rank])
        put_q(part_q, dot3(held["v"], held["pair"]), (0, 1))
        held["next"] = split(z_ref[:, rank:])
        put_q(part_q, dot3(held["v"], held["next"]), (2, 3))

    def compute_p():
        copies[3].wait()
        held["w"] = split(w_ref[...].T)
        put_l(part_p, dot3(held["w"], held["y"]))

    def compute_s():
        put_q(part_s, dot3(held["w"], held["pair"]), (0, 1))
        put_q(part_s, dot3(held["w"], held["next"]), (2, 3))

    flow_u = blocks(full_u)
    far = (x + 2) % NX

    def solve_u():
        g_own, g_other = split(whole(full_g, mine)), split(whole(full_g, others))
        q_own = table_q[pl.ds(4 * mine, 4)].reshape(rank, lanes)
        q_other = table_q[pl.ds(4 * others, 4)].reshape(rank, lanes)
        u_own, u_other = q_other, q_own
        for sweep in range(3):
            u_own, u_other = (
                q_other - dot3(g_other, split(u_other)),
                q_own - dot3(g_own, split(u_own)),
            )
        held["u"] = u_own, u_other
        full_u[x] = u_own.reshape(4, rows_q, lanes)
        run(flow_u)

    def solve_e():
        u_own, u_other = held["u"]
        p_own, p_other = split(whole(full_p, mine)), split(whole(full_p, others))
        total_s = (table_s[pl.ds(0, 4)] + table_s[pl.ds(4, 4)]).reshape(rank, lanes)
        e_slice = total_s - dot3(p_own, split(u_own)) - dot3(p_other, split(u_other))
        full_e[x] = e_slice.reshape(4, rows_q, lanes)
        held["e"] = [send(full_e.at[x], full_e.at[x], at(z, px)) for px in (right, left, far)]
        shared.append(send(full_e.at[x], sibling_e.at[x], across))

    def near_e():
        for copy, slot in zip(held["e"], (left, right)):
            copy.wait_recv()
            shared.append(send(full_e.at[slot], sibling_e.at[slot], across))

    def far_e():
        held["e"][2].wait_recv()
        shared.append(send(full_e.at[far], sibling_e.at[far], across))

    def solve_w():
        for copy in shared:
            copy.wait_recv()
        b_own, r_own = split(joined(full_e, 0)), joined(full_e, 2)
        b_sibling, r_sibling = split(joined(sibling_e, 0)), joined(sibling_e, 2)
        update = r_own
        update = r_sibling - dot3(b_sibling, split(update))
        update = r_own - dot3(b_own, split(update))
        update = r_sibling - dot3(b_sibling, split(update))
        held["update"] = split(update)

    def middle():
        y_parts = split(y_ref[...])
        pair = z_ref[:, :rank] - dot3(y_parts, split(joined(full_u, 0)))
        pair_ref[...] = pair
        pair_out = pltpu.make_async_copy(pair_ref, pair_hbm, local_sem.at[4])
        pair_out.start()
        held["m"] = pair, z_ref[:, rank:] - dot3(y_parts, split(joined(full_u, 2))), pair_out

    actions = {
        "CG": compute_g, "CQ": compute_q, "CP": compute_p, "CS": compute_s,
        "U": solve_u, "E": solve_e, "fu": lambda: run(flow_u), "en": near_e, "ef": far_e, "M": middle, "W": solve_w,
    }
    flows = {
        "xg": xg, "xq": xq, "xp": xp, "xs": xs, "zg": [zg], "zq": [zq], "zp": [zp], "zs": [zs],
        "ag": [ag], "aq": [aq], "ap": [ap], "as": [as_],
        "gn": [near(full_g, "g")], "gr": [rest(full_g, "g")], "pn": [near(full_p, "p")], "pr": [rest(full_p, "p")],
    }
    for token in ORDER:
        if token in actions:
            actions[token]()
        else:
            run(*flows[token])

    pair, middle_next, pair_out = held["m"]
    next_ref[...] = middle_next - dot3(split(pair), held["update"])
    next_out = pltpu.make_async_copy(next_ref, next_hbm, local_sem.at[5])
    next_out.start()
    for copy in sent:
        copy.wait_send()
    pair_out.wait()
    next_out.wait()


def body(low_solved, low_basis, upper_solved, upper_basis):
    rows, rank = low_solved.shape
    lanes, rows_l, rows_q = rank // 2, rank // NX // 4, rank // 4
    heights = (rows_l, rows_l, rows_q // 2, rows_q // 2)

    def blocks(*lead):
        return [pltpu.VMEM((*lead, height, lanes), F32) for height in heights]

    def pieces(*lead):
        return [pltpu.VMEM((*lead, 2, height, lanes), F32) for height in heights[:2]] + [
            pltpu.VMEM((*lead, 2, height, lanes), F32) for height in heights[2:]
        ]

    scratch = [
        pltpu.VMEM((rows, rank), F32),
        pltpu.VMEM((rows, rank), F32),
        pltpu.VMEM((rows, 2 * rank), F32),
        pltpu.VMEM((rows, rank), F32),
        pltpu.VMEM((rows, rank), F32),
        pltpu.VMEM((rows, rank), F32),
        *blocks(2, NX, 4),
        *blocks(2, 2, 4),
        *blocks(2, 4),
        *pieces(4),
        *pieces(3),
        pltpu.VMEM((NX, NZ, 2 * rows_l, lanes), F32),
        pltpu.VMEM((NX, NZ, 2 * rows_l, lanes), F32),
        pltpu.VMEM((NZ, rows_q, lanes), F32),
        pltpu.VMEM((NZ, rows_q, lanes), F32),
        pltpu.VMEM((NX, 4, rows_q, lanes), F32),
        pltpu.VMEM((NX, 4, rows_q, lanes), F32),
        pltpu.VMEM((NX, 4, rows_q, lanes), F32),
        pltpu.SemaphoreType.DMA((6,)),
        pltpu.SemaphoreType.DMA((N_MESSAGES,)),
        pltpu.SemaphoreType.DMA((N_MESSAGES,)),
    ]
    out = jax.ShapeDtypeStruct((rows, rank), F32)
    return pl.pallas_call(
        kernel,
        out_shape=(out, out),
        in_specs=[pl.BlockSpec(memory_space=pl.ANY)] * 4,
        out_specs=[pl.BlockSpec(memory_space=pl.ANY)] * 2,
        scratch_shapes=scratch,
        compiler_params=pltpu.CompilerParams(collective_id=0, has_side_effects=True, vmem_limit_bytes=60 * 2**20),
        name="lowrank_level",
    )(low_solved, low_basis, upper_solved, upper_basis)


def solution(mesh):
    spec = P(("group", "leaf"), None)
    return jax.shard_map(
        body, mesh=mesh, in_specs=(spec,) * 4, out_specs=(spec,) * 2, check_vma=False
    )
```
